768 devices in a mesh: seq: 48 (over z, x), head: 16 (over y, core).
Axes of the slice: x: 4, y: 8, z: 12, core: 2. Of those that a mesh axis runs over, the one named last changes fastest.
Arguments:
- queries: bfloat16 [24576, 8192], P('seq', 'head'), may hold values from -0.5 to 0.5
- keys: bfloat16 [24576, 8192], P('seq', 'head'), may hold values from -6 to 6
- values: bfloat16 [24576, 8192], P('seq', 'head'), may hold values from -6 to 6
- cotangent: bfloat16 [24576, 8192], P('seq', 'head'), may hold values from -6 to 6
- log_decay: float32 [64, 24576], P('head', 'seq'), may hold values from -0.6 to 0
- starts: int32 [24576], P('seq'), may hold values 0 or 1
Outputs:
- attn_out: bfloat16 [24576, 8192], P('seq', 'head')
- grad_query: bfloat16 [24576, 8192], P('seq', 'head')
- grad_key: bfloat16 [24576, 8192], P('seq', 'head')
- grad_value: bfloat16 [24576, 8192], P('seq', 'head')
The draws below stay inside these ranges and needn't reach their ends.
All inputs are finite; a program needn't handle non-finite values. No bound on the sum of `starts` on one device may be relied on, other than what follows from the above.
Results may differ from the reference program's by a relative error of at most 0.0095.
Values may be sent and summed in bfloat16 or wider, within the bound.
A program may use at most 64 MiB of HBM per device.

```python
import jax
import jax.numpy as jnp
from jax import lax

HEAD_TOTAL = 64
HEAD_DIM = 128
TOK_DEV = 512
WINDOW_TOKENS = 24576


def draw_log_decay(key, part):
    every_key = jax.random.split(key, 7)
    fast_share = 0.5
    fast_head = jax.random.uniform(every_key[0], (HEAD_TOTAL, 1)) < fast_share
    fast_rate = jnp.exp(jax.random.uniform(every_key[1], (HEAD_TOTAL, 1), minval=jnp.log(1.0 / 50.0), maxval=jnp.log(1.0 / 30.0)))
    slow_rate = jax.random.uniform(every_key[2], (HEAD_TOTAL, 1), minval=0.05, maxval=0.4) / WINDOW_TOKENS
    baseline_rate = jnp.where(fast_head, fast_rate, slow_rate)
    block_scaling = jnp.exp(jax.random.uniform(every_key[3], (HEAD_TOTAL, WINDOW_TOKENS // TOK_DEV), minval=-0.4, maxval=0.4))
    block_scaling = jnp.repeat(block_scaling, TOK_DEV, axis=1)
    jaggedness = jnp.exp(jax.random.uniform(every_key[4], (HEAD_TOTAL, WINDOW_TOKENS), minval=-0.35, maxval=0.35))
    spike_locations = jax.random.randint(every_key[5], (3,), 0, WINDOW_TOKENS)
    spike_mask = jnp.any(jnp.arange(WINDOW_TOKENS)[None, :] == spike_locations[:, None], axis=0)
    spike_penalty = jax.random.uniform(every_key[6], (HEAD_TOTAL, WINDOW_TOKENS), minval=0.2, maxval=0.35)
    spike_dropout = jnp.where(spike_mask[None, :], jnp.log(1.0 - spike_penalty), 0.0)
    return (spike_dropout - baseline_rate * block_scaling * jaggedness).astype(jnp.float32)


def place_ends(result, key, smallest, largest):
    longest = result.shape.index(max(result.shape))
    spots = []
    for shift in (0, 1):
        where = [jax.random.randint(jax.random.fold_in(key, axis), (), 0, length) for axis, length in enumerate(result.shape)]
        where[longest] = (where[longest] + shift) % result.shape[longest]
        spots.append(tuple(where))
    return result.at[spots[0]].set(smallest).at[spots[1]].set(largest)


def shard_levels(key, dims, cuts, smallest, largest):
    factor_of, own = 1.0, jax.random.fold_in(key, 6)
    for dim, blocks in cuts:
        steps = jnp.exp(jax.random.uniform(jax.random.fold_in(own, dim), (blocks,), jnp.float32, smallest / len(cuts), largest / len(cuts)))
        factor_of = factor_of * jnp.repeat(steps, dims[dim] // blocks).reshape([-1 if axis == dim else 1 for axis in range(len(dims))])
    return factor_of


def normal_values(rng, extent, scale, reach, cuts=(), kind=jnp.bfloat16):
    loudness = shard_levels(rng, extent, cuts, -0.22, 0.18) if cuts else 1.0
    drawn = jax.random.normal(rng, extent, jnp.float32) * scale * loudness
    return jnp.minimum(jnp.maximum(drawn, -reach), reach).astype(kind)


def setup_inputs(seed: int = 0) -> dict:
    arg_keys = jax.random.split(jax.random.key(seed), 7)
    return {
        "queries": normal_values(arg_keys[0], (WINDOW_TOKENS, HEAD_TOTAL * HEAD_DIM), HEAD_DIM ** -0.5, 0.5, ((0, 48), (1, 16))),
        "keys": normal_values(arg_keys[1], (WINDOW_TOKENS, HEAD_TOTAL * HEAD_DIM), 1.0, 6.0, ((0, 48), (1, 16))),
        "values": normal_values(arg_keys[2], (WINDOW_TOKENS, HEAD_TOTAL * HEAD_DIM), 1.0, 6.0, ((0, 48), (1, 16))),
        "cotangent": normal_values(arg_keys[3], (WINDOW_TOKENS, HEAD_TOTAL * HEAD_DIM), 1.0, 6.0, ((0, 48), (1, 16))),
        "log_decay": draw_log_decay(jax.random.fold_in(arg_keys[6], 71), 0),
        "starts": place_ends((jax.random.randint(arg_keys[5], (WINDOW_TOKENS,), 0, WINDOW_TOKENS // 4) < 1).astype(jnp.int32), jax.random.fold_in(arg_keys[5], 1), 0, 1),
    }


EPS = 1e-05

def rounded(array):
    return lax.optimization_barrier(array.astype(jnp.bfloat16)).astype(jnp.float32)

def block_factors(log_rates, start_flags):
    cum_log = jnp.cumsum(log_rates, axis=1)
    doc_count = jnp.cumsum(start_flags.astype(jnp.int32))
    length = start_flags.shape[0]
    position = jnp.arange(length, dtype=jnp.int32)
    inside = (position[:, None] >= position[None, :]) & (doc_count[:, None] == doc_count[None, :])
    gap = cum_log[:, :, None] - cum_log[:, None, :]
    weight = jnp.where(inside[None], jnp.exp(jnp.minimum(gap, 0.0)), 0.0)
    entering = jnp.where(doc_count[None, :] == 0, jnp.exp(cum_log), 0.0)
    leaving = jnp.where(doc_count[None, :] == doc_count[-1], jnp.exp(cum_log[:, -1:] - cum_log), 0.0)
    carried = jnp.where(doc_count[-1] == 0, jnp.exp(cum_log[:, -1]), 0.0)
    return (weight, entering, leaving, carried)

def reference(queries, keys, values, cotangent, log_decay, starts):
    token_count, row_width = queries.shape
    head_count = log_decay.shape[0]
    head_dim = row_width // head_count
    block_count = token_count // TOK_DEV

    def blocks_of(array):
        return array.reshape(block_count, TOK_DEV, head_count, head_dim)
    query_blocks = blocks_of(queries)
    key_blocks = blocks_of(keys)
    value_blocks = blocks_of(values)
    cotangent_blocks = blocks_of(cotangent)
    log_blocks = log_decay.reshape(head_count, block_count, TOK_DEV).transpose(1, 0, 2)
    start_blocks = starts.reshape(block_count, TOK_DEV)

    def forward(state, pieces):
        query_head, key_head, value_head, cotangent_head, log_rates, start_flags = pieces
        weight, entering, leaving, carried = block_factors(log_rates, start_flags)
        query_wide = query_head.astype(jnp.float32)
        key_wide = key_head.astype(jnp.float32)
        value_wide = value_head.astype(jnp.float32)
        cotangent_wide = cotangent_head.astype(jnp.float32)
        weights_rounded = rounded(jnp.einsum('thd,shd->hts', query_wide, key_wide) * weight)
        state_rounded = rounded(state)
        outputs = jnp.einsum('hts,shd->thd', weights_rounded, value_wide)
        outputs = outputs + entering.T[:, :, None] * jnp.einsum('thd,hde->the', query_wide, state_rounded)
        keys_decayed = rounded(leaving.T[:, :, None] * key_wide)
        update = rounded(jnp.einsum('shd,she->hde', keys_decayed, value_wide))
        inverse_scale = lax.rsqrt(lax.optimization_barrier(jnp.sum(outputs * outputs, axis=(1, 2))) / row_width + EPS)
        attn_block = (outputs * inverse_scale[:, None, None]).astype(jnp.bfloat16)
        grad_sum = lax.optimization_barrier(jnp.sum(cotangent_wide * outputs, axis=(1, 2)))
        cubed = inverse_scale * inverse_scale * inverse_scale
        grad_out = rounded(inverse_scale[:, None, None] * cotangent_wide - (cubed * grad_sum / row_width)[:, None, None] * outputs)
        queries_decayed = rounded(entering.T[:, :, None] * query_wide)
        grad_state = rounded(jnp.einsum('thd,the->hde', queries_decayed, grad_out))
        next_state = carried[:, None, None] * state + update
        return (next_state, (attn_block, grad_out.astype(jnp.bfloat16), state_rounded, grad_state, carried))
    initial = jnp.zeros((head_count, head_dim, head_dim), jnp.float32)
    final_state, stacked = lax.scan(forward, initial, (query_blocks, key_blocks, value_blocks, cotangent_blocks, log_blocks, start_blocks))
    attn_blocks, grad_out_blocks, state_blocks, grad_states, carry_blocks = stacked

    def backward_carry(back, pieces):
        grad_state, carried = pieces
        return (grad_state + carried[:, None, None] * back, back)
    final_back, back_blocks = lax.scan(backward_carry, initial, (grad_states, carry_blocks), reverse=True)

    def backward(pieces):
        query_head, key_head, value_head, log_rates, start_flags, grad_out, state_rounded, back = pieces
        weight, entering, leaving, carried = block_factors(log_rates, start_flags)
        query_wide = query_head.astype(jnp.float32)
        key_wide = key_head.astype(jnp.float32)
        value_wide = value_head.astype(jnp.float32)
        grad_wide = grad_out.astype(jnp.float32)
        weights_rounded = rounded(jnp.einsum('thd,shd->hts', query_wide, key_wide) * weight)
        grads_rounded = rounded(jnp.einsum('thd,shd->hts', grad_wide, value_wide) * weight)
        back_rounded = rounded(back)
        grad_query = jnp.einsum('hts,shd->thd', grads_rounded, key_wide)
        grad_query = grad_query + entering.T[:, :, None] * jnp.einsum('the,hde->thd', grad_wide, state_rounded)
        grad_key = jnp.einsum('hts,thd->shd', grads_rounded, query_wide)
        grad_key = grad_key + leaving.T[:, :, None] * jnp.einsum('she,hde->shd', value_wide, back_rounded)
        grad_value = jnp.einsum('hts,thd->shd', weights_rounded, grad_wide)
        grad_value = grad_value + leaving.T[:, :, None] * jnp.einsum('shd,hde->she', key_wide, back_rounded)
        return (grad_query.astype(jnp.bfloat16), grad_key.astype(jnp.bfloat16), grad_value.astype(jnp.bfloat16))
    grad_query, grad_key, grad_value = lax.map(backward, (query_blocks, key_blocks, value_blocks, log_blocks, start_blocks, grad_out_blocks, state_blocks, back_blocks))
    return (attn_blocks.reshape(token_count, row_width), grad_query.reshape(token_count, row_width), grad_key.reshape(token_count, row_width), grad_value.reshape(token_count, row_width))
```

```python
import functools

import jax
import jax.numpy as jnp
from jax import lax
from jax.experimental import pallas as pl
from jax.experimental.pallas import tpu as pltpu
from jax.sharding import PartitionSpec as P

HEADS = 4
DIM = 128
TOK = 512
CH = 128
NCH = TOK // CH
XN = 4
EPS = 1e-05
MESH = pl.DeviceIdType.MESH
F32 = jnp.float32
BF16 = jnp.bfloat16
NT = (((1,), (1,)), ((), ()))
TN = (((0,), (0,)), ((), ()))


def mm(a, b, dims=None):
    if dims is None:
        return jnp.dot(a, b, preferred_element_type=F32)
    return lax.dot_general(a, b, dims, preferred_element_type=F32)


def kernel(
    zn, hn,
    q_hbm, k_hbm, v_hbm, c_hbm, ld_ref, st_ref,
    attn_hbm, gq_hbm, gk_hbm, gv_hbm,
    q, k, v, cot, attn_s, gq_s, gk_s, gv_s,
    s16, lrow, enr, ler, lb, eb, leb, bias, wt, pp, dpp, o_s, gs, qd, gkp, gvp,
    acc_s, acc_g, invb, cfb,
    cb, crx, arow, aoff, coef,
    ub, rx, tf, z1s, z1r, z2s, z2r, w3, sts, str_,
    hs_s, hs_r,
    in_sem, out_sem, c_ss, c_rs, a_ss, a_rs, u_ss, u_rs, z1_ss, z1_rs, z2_ss, z2_rs, x_ss, x_rs, h_ss, h_rs,
):
    full_width = hn * HEADS * DIM
    me = lax.axis_index("seq")
    hd = lax.axis_index("head")
    z = lax.div(me, XN)
    x = lax.rem(me, XN)
    near = [d for d in (1, 2, 3) if d < zn]
    far = [d for d in range(4, zn, 4)]

    def xdev(d):
        return {"seq": z * XN + lax.rem(x + d, XN)}

    def zdev(d):
        return {"seq": lax.rem(z + d, zn) * XN + x}

    def hdev(d):
        return {"head": lax.rem(hd + d, hn)}

    def send(src, dst, ss, rs, dev):
        return pltpu.make_async_remote_copy(
            src_ref=src, dst_ref=dst, send_sem=ss, recv_sem=rs, device_id=dev, device_id_type=MESH
        )

    loads = [
        pltpu.make_async_copy(s, d, in_sem.at[n])
        for n, (s, d) in enumerate(((k_hbm, k), (v_hbm, v), (q_hbm, q), (c_hbm, cot)))
    ]
    for copy in loads:
        copy.start()

    barrier = pltpu.get_barrier_semaphore()
    for d in range(1, XN):
        pl.semaphore_signal(barrier, inc=1, device_id=xdev(d), device_id_type=MESH)
    for d in range(1, zn):
        pl.semaphore_signal(barrier, inc=1, device_id=zdev(d), device_id_type=MESH)
    for d in range(1, hn):
        pl.semaphore_signal(barrier, inc=1, device_id=hdev(d), device_id_type=MESH)

    s16[0:HEADS, :] = ld_ref[...]
    s16[4:5, :] = st_ref[...].astype(F32)
    s16[5:8, :] = jnp.zeros((3, TOK), F32)
    sums = s16[0:8, :]
    lane = lax.broadcasted_iota(jnp.int32, (8, TOK), 1)
    shift = 1
    while shift < TOK:
        sums = sums + jnp.where(lane >= shift, pltpu.roll(sums, shift, 1), 0.0)
        shift *= 2
    lsum = sums[0:HEADS, :]
    count = sums[4:5, :]
    last = sums[:, TOK - 1 : TOK]
    enter = jnp.where(count == 0.0, jnp.exp(lsum), 0.0)
    leave = jnp.where(count == last[4:5], jnp.exp(last[0:HEADS] - lsum), 0.0)
    s16[0:8, :] = sums
    s16[8:12, :] = enter
    s16[12:16, :] = leave
    for h in range(HEADS):
        lrow[h] = lsum[h : h + 1, :]
        enr[h] = enter[h : h + 1, :]
        ler[h] = leave[h : h + 1, :]
        cb[h] = jnp.broadcast_to(enter[h : h + 1, TOK - 1 : TOK], (1, DIM))

    pl.semaphore_wait(barrier, (XN - 1) + (zn - 1) + (hn - 1))

    def c_copy(d):
        return send(cb.at[lax.rem(x + d, XN)], crx.at[x], c_ss.at[d - 1], c_rs.at[d - 1], xdev(d))

    for d in (2, 1, 3):
        c_copy(d).start()
    crx[x] = cb[x]

    def x_copy(src, dst, ss, rs, d):
        return send(src.at[lax.rem(x + d, XN)], dst.at[x], ss.at[d - 1], rs.at[d - 1], xdev(d))

    def x_arrive(src, dst, ss, rs, d):
        come = lax.rem(x + XN - d, XN)
        send(src.at[come], dst.at[come], ss.at[d - 1], rs.at[d - 1], xdev(d)).wait_recv()

    def cols(h):
        return pl.ds(pl.multiple_of(h * DIM, DIM), DIM)

    loads[0].wait()
    loads[1].wait()

    for d in (2, 1, 3, 0):
        h = lax.rem(x + d, XN)
        kt = k[:, cols(h)].astype(F32).T
        kdec = (kt * ler[h]).astype(BF16)
        ub[0, h] = mm(kdec, v[:, cols(h)]).astype(BF16)
        if d:
            x_copy(ub.at[0], rx.at[0], u_ss.at[0], u_rs.at[0], d).start()
        else:
            rx[0, h] = ub[0, h]

    for d in range(1, XN):
        come = lax.rem(x + XN - d, XN)
        send(cb.at[come], crx.at[come], c_ss.at[d - 1], c_rs.at[d - 1], xdev(d)).wait_recv()
    arow[0] = (crx[0] * crx[1]) * (crx[2] * crx[3])

    def a_copy(d):
        return send(arow.at[0], aoff.at[d - 1], a_ss.at[d - 1], a_rs.at[d - 1], zdev(d))

    for d in range(1, zn):
        a_copy(d).start()

    columns = s16[...].T
    for h in range(HEADS):
        lb[h] = jnp.broadcast_to(columns[:, h : h + 1], (TOK, DIM))
        eb[h] = jnp.broadcast_to(columns[:, 8 + h : 9 + h], (TOK, DIM))
        leb[h] = jnp.broadcast_to(columns[:, 12 + h : 13 + h], (TOK, DIM))
    row_pos = lax.broadcasted_iota(jnp.int32, (TOK, TOK), 0)
    col_pos = lax.broadcasted_iota(jnp.int32, (TOK, TOK), 1)
    inside = (row_pos >= col_pos) & (columns[:, 4:5] == s16[4:5, :])
    bias[...] = jnp.where(inside, 0.0, -1e30)
    loads[2].wait()

    def intra(h, carry):
        qt = q[:, cols(h)].astype(F32).T
        qd[h] = (qt * enr[h]).astype(BF16)
        for i in range(NCH):
            rows = slice(i * CH, (i + 1) * CH)
            wide = (i + 1) * CH
            scores = mm(q[rows, cols(h)], k[0:wide, cols(h)], NT)
            for j in range(i + 1):
                part = slice(j * CH, (j + 1) * CH)
                gap = jnp.minimum(lb[h, rows, :] - lrow[h, :, part], 0.0)
                weight = jnp.exp(gap + bias[rows, part])
                wt[h, rows, part] = weight
                pp[h, rows, part] = (scores[:, part] * weight).astype(BF16)
            o_s[rows, cols(h)] = mm(pp[h, rows, 0:wide], v[0:wide, cols(h)])
        return carry

    def row_total(n):
        if n == 0:
            total = rx[n, 0].astype(F32)
            for i in range(1, XN):
                total = total * crx[i] + rx[n, i].astype(F32)
        else:
            total = rx[n, XN - 1].astype(F32)
            for i in range(XN - 2, -1, -1):
                total = total * crx[i] + rx[n, i].astype(F32)
        return total

    def z_target(n, d):
        return zdev(d) if n == 0 else zdev(zn - d)

    def z1_copy(n, d):
        i = near.index(d)
        return send(z1s.at[n], z1r.at[n, i], z1_ss.at[n, i], z1_rs.at[n, i], z_target(n, d))

    def z2_copy(n, d):
        i = far.index(d)
        return send(z2s.at[n], z2r.at[n, i], z2_ss.at[n, i], z2_rs.at[n, i], z_target(n, d))

    def scan_start(n):
        for d in (1, 3, 2):
            x_arrive(ub.at[n], rx.at[n], u_ss.at[n], u_rs.at[n], d)
        total = row_total(n)
        tf[...] = total
        z1s[n] = total.astype(BF16)
        for d in near[::-1]:
            z1_copy(n, d).start()

    def scan_middle(n):
        window = jnp.zeros((DIM, DIM), F32)
        for d in near:
            z1_copy(n, d).wait_recv()
            window = window + coef[n, d] * z1r[n, near.index(d)].astype(F32)
        w3[...] = window
        if far:
            z2s[n] = (tf[...] + arow[0] * window).astype(BF16)
            for d in far:
                z2_copy(n, d).start()

    def scan_end(n):
        state = w3[...]
        for d in far:
            z2_copy(n, d).wait_recv()
            state = state + coef[n, d] * z2r[n, far.index(d)].astype(F32)
        order = range(XN) if n == 0 else range(XN - 1, -1, -1)
        for i in order:
            sts[n, i] = state.astype(BF16)
            state = state * crx[i] + rx[n, i].astype(F32)
        for d in (2, 1, 3):
            x_copy(sts.at[n], str_.at[n], x_ss.at[n], x_rs.at[n], d).start()
        str_[n, x] = sts[n, x]

    def state_arrive(n, d):
        if d:
            x_arrive(sts.at[n], str_.at[n], x_ss.at[n], x_rs.at[n], d)

    lax.fori_loop(0, 1, intra, 0)
    scan_start(0)
    lax.fori_loop(1, 3, intra, 0)

    for d in range(1, zn):
        a_copy(d).wait_recv()
    for n in range(2):
        product = jnp.ones((1, DIM), F32)
        for d in range(1, zn):
            ok = (z >= d) if n == 0 else (z + d < zn)
            coef[n, d] = jnp.where(ok, product, 0.0)
            product = product * (aoff[d - 1] if n == 0 else aoff[zn - d - 1])

    scan_middle(0)
    lax.fori_loop(3, HEADS, intra, 0)
    loads[3].wait()
    scan_end(0)

    for d in (0, 1, 3, 2):
        state_arrive(0, d)
        h = lax.rem(x + XN - d, XN)
        for i in range(NCH):
            rows = slice(i * CH, (i + 1) * CH)
            out = o_s[rows, cols(h)] + eb[h, rows, :] * mm(q[rows, cols(h)], str_[0, h])
            o_s[rows, cols(h)] = out
            square = out * out
            along = out * cot[rows, cols(h)].astype(F32)
            if d == 0:
                acc_s[rows, :] = square
                acc_g[rows, :] = along
            else:
                acc_s[rows, :] += square
                acc_g[rows, :] += along
    square_row = jnp.sum(acc_s[...].T, axis=0, keepdims=True)
    along_row = jnp.sum(acc_g[...].T, axis=0, keepdims=True)
    for i in range(NCH):
        hs_s[i : i + 1, :] = square_row[:, i * CH : (i + 1) * CH]
        hs_s[4 + i : 5 + i, :] = along_row[:, i * CH : (i + 1) * CH]

    def h_copy(d):
        return send(hs_s, hs_r.at[d - 1], h_ss.at[d - 1], h_rs.at[d - 1], hdev(d))

    for d in range(1, hn):
        h_copy(d).start()
    both = hs_s[...]
    for d in range(1, hn):
        h_copy(d).wait_recv()
        both = both + hs_r[d - 1]
    inverse = lax.rsqrt(both[0:4] / full_width + EPS)
    cubed = inverse * inverse * inverse
    second = cubed * both[4:8] / full_width
    flat = jnp.concatenate([inverse, second], axis=0).T
    for i in range(NCH):
        rows = slice(i * CH, (i + 1) * CH)
        invb[rows, :] = jnp.broadcast_to(flat[:, i : i + 1], (CH, DIM))
        cfb[rows, :] = jnp.broadcast_to(flat[:, 4 + i : 5 + i], (CH, DIM))

    for d in (2, 1, 3, 0):
        h = lax.rem(x + d, XN)
        for i in range(NCH):
            rows = slice(i * CH, (i + 1) * CH)
            gs[rows, cols(h)] = (
                invb[rows, :] * cot[rows, cols(h)].astype(F32) - cfb[rows, :] * o_s[rows, cols(h)]
            ).astype(BF16)
        ub[1, h] = mm(qd[h], gs[:, cols(h)]).astype(BF16)
        if d:
            x_copy(ub.at[1], rx.at[1], u_ss.at[1], u_rs.at[1], d).start()
        else:
            rx[1, h] = ub[1, h]

    def out_copy(n, h):
        src, dst = ((attn_s, attn_hbm), (gq_s, gq_hbm), (gk_s, gk_hbm), (gv_s, gv_hbm))[n]
        return pltpu.make_async_copy(src.at[:, cols(h)], dst.at[:, cols(h)], out_sem.at[n, h])

    def local_back(h, carry):
        for i in range(NCH):
            rows = slice(i * CH, (i + 1) * CH)
            wide = (i + 1) * CH
            attn_s[rows, cols(h)] = (o_s[rows, cols(h)] * invb[rows, :]).astype(BF16)
            inner = mm(gs[rows, cols(h)], v[0:wide, cols(h)], NT)
            dpp[rows, 0:wide] = (inner * wt[h, rows, 0:wide]).astype(BF16)
            grad = mm(dpp[rows, 0:wide], k[0:wide, cols(h)])
            grad = grad + eb[h, rows, :] * mm(gs[rows, cols(h)], str_[0, h], NT)
            gq_s[rows, cols(h)] = grad.astype(BF16)
        out_copy(0, h).start()
        out_copy(1, h).start()
        for j in range(NCH):
            part = slice(j * CH, (j + 1) * CH)
            gkp[part, cols(h)] = mm(dpp[j * CH :, part], q[j * CH :, cols(h)], TN)
            gvp[part, cols(h)] = mm(pp[h, j * CH :, part], gs[j * CH :, cols(h)], TN)
        return carry

    lax.fori_loop(0, 1, local_back, 0)
    scan_start(1)
    lax.fori_loop(1, 3, local_back, 0)
    scan_middle(1)
    lax.fori_loop(3, HEADS, local_back, 0)
    scan_end(1)

    for d in (0, 1, 3, 2):
        state_arrive(1, d)
        h = lax.rem(x + XN - d, XN)
        for j in range(NCH):
            part = slice(j * CH, (j + 1) * CH)
            gk_s[part, cols(h)] = (
                gkp[part, cols(h)] + leb[h, part, :] * mm(v[part, cols(h)], str_[1, h], NT)
            ).astype(BF16)
            gv_s[part, cols(h)] = (
                gvp[part, cols(h)] + leb[h, part, :] * mm(k[part, cols(h)], str_[1, h])
            ).astype(BF16)
        out_copy(2, h).start()
        out_copy(3, h).start()

    for d in range(1, XN):
        c_copy(d).wait_send()
        for n in range(2):
            x_copy(ub.at[n], rx.at[n], u_ss.at[n], u_rs.at[n], d).wait_send()
            x_copy(sts.at[n], str_.at[n], x_ss.at[n], x_rs.at[n], d).wait_send()
    for d in range(1, zn):
        a_copy(d).wait_send()
    for d in range(1, hn):
        h_copy(d).wait_send()
    for n in range(2):
        for d in near:
            z1_copy(n, d).wait_send()
        for d in far:
            z2_copy(n, d).wait_send()
    for n in range(4):
        for h in range(HEADS):
            out_copy(n, h).wait()


def solution(mesh):
    zn = mesh.shape["seq"] // XN
    hn = mesh.shape["head"]
    near = max(min(3, zn - 1), 1)
    far = max(len(range(4, zn, 4)), 1)
    dma = pltpu.SemaphoreType.DMA

    def per_device(queries, keys, values, cotangent, log_decay, starts):
        big = pltpu.VMEM((TOK, HEADS * DIM), BF16)
        bigf = pltpu.VMEM((TOK, HEADS * DIM), F32)
        col = pltpu.VMEM((HEADS, TOK, DIM), F32)
        row = pltpu.VMEM((HEADS, 1, TOK), F32)
        mat = (DIM, DIM)
        scratch = [
            big, big, big, big, big, big, big, big,
            pltpu.VMEM((16, TOK), F32), row, row, row, col, col, col,
            pltpu.VMEM((TOK, TOK), F32),
            pltpu.VMEM((HEADS, TOK, TOK), F32),
            pltpu.VMEM((HEADS, TOK, TOK), BF16),
            pltpu.VMEM((TOK, TOK), BF16),
            bigf, big, pltpu.VMEM((HEADS, DIM, TOK), BF16), bigf, bigf,
            pltpu.VMEM((TOK, DIM), F32), pltpu.VMEM((TOK, DIM), F32),
            pltpu.VMEM((TOK, DIM), F32), pltpu.VMEM((TOK, DIM), F32),
            pltpu.VMEM((HEADS, 1, DIM), F32), pltpu.VMEM((XN, 1, DIM), F32),
            pltpu.VMEM((1, 1, DIM), F32), pltpu.VMEM((max(zn - 1, 1), 1, DIM), F32),
            pltpu.VMEM((2, zn, 1, DIM), F32),
            pltpu.VMEM((2, HEADS) + mat, BF16), pltpu.VMEM((2, XN) + mat, BF16),
            pltpu.VMEM(mat, F32),
            pltpu.VMEM((2,) + mat, BF16), pltpu.VMEM((2, near) + mat, BF16),
            pltpu.VMEM((2,) + mat, BF16), pltpu.VMEM((2, far) + mat, BF16),
            pltpu.VMEM(mat, F32),
            pltpu.VMEM((2, XN) + mat, BF16), pltpu.VMEM((2, HEADS) + mat, BF16),
            pltpu.VMEM((8, DIM), F32), pltpu.VMEM((max(hn - 1, 1), 8, DIM), F32),
            dma((4,)), dma((4, HEADS)),
            dma((3,)), dma((3,)),
            dma((max(zn - 1, 1),)), dma((max(zn - 1, 1),)),
            dma((2, 3)), dma((2, 3)),
            dma((2, near)), dma((2, near)),
            dma((2, far)), dma((2, far)),
            dma((2, 3)), dma((2, 3)),
            dma((max(hn - 1, 1),)), dma((max(hn - 1, 1),)),
        ]
        out = jax.ShapeDtypeStruct(queries.shape, BF16)
        hbm = pl.BlockSpec(memory_space=pl.ANY)
        vmem = pl.BlockSpec(memory_space=pltpu.VMEM)
        return pl.pallas_call(
            functools.partial(kernel, zn, hn),
            out_shape=(out, out, out, out),
            in_specs=[hbm, hbm, hbm, hbm, vmem, vmem],
            out_specs=(hbm, hbm, hbm, hbm),
            scratch_shapes=scratch,
            compiler_params=pltpu.CompilerParams(
                collective_id=0, has_side_effects=True, vmem_limit_bytes=60 * 1024 * 1024
            ),
        )(queries, keys, values, cotangent, log_decay, starts.reshape(1, TOK))

    in_specs = (
        P("seq", "head"),
        P("seq", "head"),
        P("seq", "head"),
        P("seq", "head"),
        P("head", "seq"),
        P("seq"),
    )
    out_specs = (P("seq", "head"), P("seq", "head"), P("seq", "head"), P("seq", "head"))
    return jax.shard_map(
        per_device, mesh=mesh, in_specs=in_specs, out_specs=out_specs, check_vma=False
    )
```

```python
import functools

import jax
import jax.numpy as jnp
from jax import lax
from jax.experimental import pallas as pl
from jax.experimental.pallas import tpu as pltpu
from jax.sharding import PartitionSpec as P

HEADS = 4
DIM = 128
TOK = 512
CH = 128
NCH = TOK // CH
XN = 4
PARTS = 2
PR = DIM // PARTS
EPS = 1e-05
MESH = pl.DeviceIdType.MESH
F32 = jnp.float32
BF16 = jnp.bfloat16
NT = (((1,), (1,)), ((), ()))
TN = (((0,), (0,)), ((), ()))


def mm(a, b, dims=None):
    if dims is None:
        return jnp.dot(a, b, preferred_element_type=F32)
    return lax.dot_general(a, b, dims, preferred_element_type=F32)


def kernel(
    zn, hn,
    q_hbm, k_hbm, v_hbm, c_hbm, ld_hbm, st_hbm,
    attn_s, gq_s, gk_s, gv_s,
    q, k, v, cot, ld_ref, st_ref,
    s16, lrow, enr, ler, lb, eb, leb, bias, wt, pp, dpp, o_s, gs, qd, gkp, gvp,
    acc_s, acc_g, invb, cfb,
    cb, crx, arow, aoff, coef,
    ub, rx, tf, z1s, z1r, z2s, z2r, w3, sts, str_,
    hs_s, hs_r,
    in_sem, c_ss, c_rs, a_ss, a_rs, u_ss, u_rs, z1_ss, z1_rs, z2_ss, z2_rs, x_ss, x_rs, h_ss, h_rs,
):
    full_width = hn * HEADS * DIM
    me = lax.axis_index("seq")
    hd = lax.axis_index("head")
    z = lax.div(me, XN)
    x = lax.rem(me, XN)
    near = [d for d in (1, 2, 3) if d < zn]
    far = [d for d in range(4, zn, 4)]

    def xdev(d):
        return {"seq": z * XN + lax.rem(x + d, XN)}

    def zdev(d):
        return {"seq": lax.rem(z + d, zn) * XN + x}

    def hdev(d):
        return {"head": lax.rem(hd + d, hn)}

    def send(src, dst, ss, rs, dev):
        return pltpu.make_async_remote_copy(
            src_ref=src, dst_ref=dst, send_sem=ss, recv_sem=rs, device_id=dev, device_id_type=MESH
        )

    barrier = pltpu.get_barrier_semaphore()
    for d in range(1, XN):
        pl.semaphore_signal(barrier, inc=1, device_id=xdev(d), device_id_type=MESH)
    for d in range(1, zn):
        pl.semaphore_signal(barrier, inc=1, device_id=zdev(d), device_id_type=MESH)
    for d in range(1, hn):
        pl.semaphore_signal(barrier, inc=1, device_id=hdev(d), device_id_type=MESH)

    loads = [
        pltpu.make_async_copy(s, d, in_sem.at[n])
        for n, (s, d) in enumerate(((ld_hbm, ld_ref), (st_hbm, st_ref), (k_hbm, k), (v_hbm, v), (q_hbm, q), (c_hbm, cot)))
    ]
    for copy in loads:
        copy.start()

    loads[0].wait()
    loads[1].wait()
    s16[0:HEADS, :] = ld_ref[...]
    s16[4:5, :] = st_ref[...].astype(F32)
    s16[5:8, :] = jnp.zeros((3, TOK), F32)
    sums = s16[0:8, :]
    lane = lax.broadcasted_iota(jnp.int32, (8, TOK), 1)
    shift = 1
    while shift < TOK:
        sums = sums + jnp.where(lane >= shift, pltpu.roll(sums, shift, 1), 0.0)
        shift *= 2
    lsum = sums[0:HEADS, :]
    count = sums[4:5, :]
    last = sums[:, TOK - 1 : TOK]
    enter = jnp.where(count == 0.0, jnp.exp(lsum), 0.0)
    leave = jnp.where(count == last[4:5], jnp.exp(last[0:HEADS] - lsum), 0.0)
    s16[0:8, :] = sums
    s16[8:12, :] = enter
    s16[12:16, :] = leave
    for h in range(HEADS):
        lrow[h] = lsum[h : h + 1, :]
        enr[h] = enter[h : h + 1, :]
        ler[h] = leave[h : h + 1, :]
        cb[h] = jnp.broadcast_to(enter[h : h + 1, TOK - 1 : TOK], (1, DIM))

    pl.semaphore_wait(barrier, (XN - 1) + (zn - 1) + (hn - 1))

    def c_copy(d):
        return send(cb.at[lax.rem(x + d, XN)], crx.at[x], c_ss.at[d - 1], c_rs.at[d - 1], xdev(d))

    for d in (2, 1, 3):
        c_copy(d).start()
    crx[x] = cb[x]

    def chunk(c):
        return slice(c * PR, (c + 1) * PR)

    def x_copy(src, dst, ss, rs, n, c, d):
        return send(
            src.at[n, lax.rem(x + d, XN), chunk(c)], dst.at[n, x, chunk(c)],
            ss.at[n, c, d - 1], rs.at[n, c, d - 1], xdev(d),
        )

    def x_arrive(src, dst, ss, rs, n, c, d):
        come = lax.rem(x + XN - d, XN)
        send(
            src.at[n, come, chunk(c)], dst.at[n, come, chunk(c)],
            ss.at[n, c, d - 1], rs.at[n, c, d - 1], xdev(d),
        ).wait_recv()

    def cols(h):
        return pl.ds(pl.multiple_of(h * DIM, DIM), DIM)

    loads[2].wait()
    loads[3].wait()

    for d in (2, 1, 3, 0):
        h = lax.rem(x + d, XN)
        kt = k[:, cols(h)].astype(F32).T
        kdec = (kt * ler[h]).astype(BF16)
        ub[0, h] = mm(kdec, v[:, cols(h)]).astype(BF16)
        if d:
            x_copy(ub, rx, u_ss, u_rs, 0, 0, d).start()
        else:
            rx[0, h] = ub[0, h]
    for c in range(1, PARTS):
        for d in (2, 1, 3):
            x_copy(ub, rx, u_ss, u_rs, 0, c, d).start()

    columns = s16[...].T
    for h in range(HEADS):
        lb[h] = jnp.broadcast_to(columns[:, h : h + 1], (TOK, DIM))
        eb[h] = jnp.broadcast_to(columns[:, 8 + h : 9 + h], (TOK, DIM))
        leb[h] = jnp.broadcast_to(columns[:, 12 + h : 13 + h], (TOK, DIM))
    row_pos = lax.broadcasted_iota(jnp.int32, (TOK, TOK), 0)
    col_pos = lax.broadcasted_iota(jnp.int32, (TOK, TOK), 1)
    inside = (row_pos >= col_pos) & (columns[:, 4:5] == s16[4:5, :])
    bias[...] = jnp.where(inside, 0.0, -1e30)
    loads[4].wait()

    def intra(h, carry):
        qt = q[:, cols(h)].astype(F32).T
        qd[h] = (qt * enr[h]).astype(BF16)
        for i in range(NCH):
            rows = slice(i * CH, (i + 1) * CH)
            wide = (i + 1) * CH
            scores = mm(q[rows, cols(h)], k[0:wide, cols(h)], NT)
            for j in range(i + 1):
                part = slice(j * CH, (j + 1) * CH)
                gap = jnp.minimum(lb[h, rows, :] - lrow[h, :, part], 0.0)
                weight = jnp.exp(gap + bias[rows, part])
                wt[h, rows, part] = weight
                pp[h, rows, part] = (scores[:, part] * weight).astype(BF16)
            o_s[rows, cols(h)] = mm(pp[h, rows, 0:wide], v[0:wide, cols(h)])
        return carry

    def row_total(n, c):
        rs = chunk(c)
        order = range(XN) if n == 0 else range(XN - 1, -1, -1)
        total = None
        for i in order:
            term = rx[n, i, rs].astype(F32)
            total = term if total is None else total * crx[i] + term
        return total

    def z_target(n, d):
        return zdev(d) if n == 0 else zdev(zn - d)

    def to_later(n, d):
        return pl.when(z + d < zn) if n == 0 else pl.when(z >= d)

    def from_earlier(n, d):
        return pl.when(z >= d) if n == 0 else pl.when(z + d < zn)

    def z1_copy(n, c, d):
        i = near.index(d)
        return send(
            z1s.at[n, chunk(c)], z1r.at[n, i, chunk(c)], z1_ss.at[n, c, i], z1_rs.at[n, c, i], z_target(n, d)
        )

    def z2_copy(n, c, d):
        i = far.index(d)
        return send(
            z2s.at[n, chunk(c)], z2r.at[n, i, chunk(c)], z2_ss.at[n, c, i], z2_rs.at[n, c, i], z_target(n, d)
        )

    def scan_start(n, c):
        for d in (1, 3, 2):
            x_arrive(ub, rx, u_ss, u_rs, n, c, d)
        total = row_total(n, c)
        tf[chunk(c)] = total
        z1s[n, chunk(c)] = total.astype(BF16)
        for d in near[::-1]:
            @to_later(n, d)
            def _():
                z1_copy(n, c, d).start()

    def scan_middle(n, c):
        w3[chunk(c)] = jnp.zeros((PR, DIM), F32)
        for d in near:
            @from_earlier(n, d)
            def _():
                z1_copy(n, c, d).wait_recv()
                w3[chunk(c)] += coef[n, d] * z1r[n, near.index(d), chunk(c)].astype(F32)
        if far:
            z2s[n, chunk(c)] = (tf[chunk(c)] + arow[0] * w3[chunk(c)]).astype(BF16)
        for d in far:
            @to_later(n, d)
            def _():
                z2_copy(n, c, d).start()

    def scan_end(n, c):
        for d in far:
            @from_earlier(n, d)
            def _():
                z2_copy(n, c, d).wait_recv()
                w3[chunk(c)] += coef[n, d] * z2r[n, far.index(d), chunk(c)].astype(F32)
        state = w3[chunk(c)]
        order = range(XN) if n == 0 else range(XN - 1, -1, -1)
        for i in order:
            sts[n, i, chunk(c)] = state.astype(BF16)
            state = state * crx[i] + rx[n, i, chunk(c)].astype(F32)
        for d in (2, 1, 3):
            x_copy(sts, str_, x_ss, x_rs, n, c, d).start()
        str_[n, x, chunk(c)] = sts[n, x, chunk(c)]

    def state_arrive(n, d):
        if d:
            for c in range(PARTS):
                x_arrive(sts, str_, x_ss, x_rs, n, c, d)

    lax.fori_loop(0, 1, intra, 0)
    for d in range(1, XN):
        come = lax.rem(x + XN - d, XN)
        send(cb.at[come], crx.at[come], c_ss.at[d - 1], c_rs.at[d - 1], xdev(d)).wait_recv()
    arow[0] = (crx[0] * crx[1]) * (crx[2] * crx[3])

    def a_copy(d):
        return send(arow.at[0], aoff.at[d - 1], a_ss.at[d - 1], a_rs.at[d - 1], zdev(d))

    for d in sorted(range(1, zn), key=lambda d: min(d, zn - d), reverse=True):
        a_copy(d).start()

    for c in range(PARTS):
        scan_start(0, c)
    lax.fori_loop(1, HEADS, intra, 0)
    for d in range(1, zn):
        a_copy(d).wait_recv()
    for n in range(2):
        product = jnp.ones((1, DIM), F32)
        for d in range(1, zn):
            coef[n, d] = product
            product = product * (aoff[d - 1] if n == 0 else aoff[zn - d - 1])
    for c in range(PARTS):
        scan_middle(0, c)
    loads[5].wait()
    for c in range(PARTS):
        scan_end(0, c)
    for d in (0, 1, 3, 2):
        state_arrive(0, d)
        h = lax.rem(x + XN - d, XN)
        for i in range(NCH):
            rows = slice(i * CH, (i + 1) * CH)
            out = o_s[rows, cols(h)] + eb[h, rows, :] * mm(q[rows, cols(h)], str_[0, h])
            o_s[rows, cols(h)] = out
            square = out * out
            along = out * cot[rows, cols(h)].astype(F32)
            if d == 0:
                acc_s[rows, :] = square
                acc_g[rows, :] = along
            else:
                acc_s[rows, :] += square
                acc_g[rows, :] += along
    square_row = jnp.sum(acc_s[...].T, axis=0, keepdims=True)
    along_row = jnp.sum(acc_g[...].T, axis=0, keepdims=True)
    for i in range(NCH):
        hs_s[i : i + 1, :] = square_row[:, i * CH : (i + 1) * CH]
        hs_s[4 + i : 5 + i, :] = along_row[:, i * CH : (i + 1) * CH]

    def h_copy(d):
        return send(hs_s, hs_r.at[d - 1], h_ss.at[d - 1], h_rs.at[d - 1], hdev(d))

    for d in sorted(range(1, hn), key=lambda d: min(d, hn - d), reverse=True):
        h_copy(d).start()
    both = hs_s[...]
    for d in range(1, hn):
        h_copy(d).wait_recv()
        both = both + hs_r[d - 1]
    inverse = lax.rsqrt(both[0:4] / full_width + EPS)
    cubed = inverse * inverse * inverse
    second = cubed * both[4:8] / full_width
    flat = jnp.concatenate([inverse, second], axis=0).T
    for i in range(NCH):
        rows = slice(i * CH, (i + 1) * CH)
        invb[rows, :] = jnp.broadcast_to(flat[:, i : i + 1], (CH, DIM))
        cfb[rows, :] = jnp.broadcast_to(flat[:, 4 + i : 5 + i], (CH, DIM))

    for d in (2, 1, 3, 0):
        h = lax.rem(x + d, XN)
        for i in range(NCH):
            rows = slice(i * CH, (i + 1) * CH)
            gs[rows, cols(h)] = (
                invb[rows, :] * cot[rows, cols(h)].astype(F32) - cfb[rows, :] * o_s[rows, cols(h)]
            ).astype(BF16)
        ub[1, h] = mm(qd[h], gs[:, cols(h)]).astype(BF16)
        if d:
            x_copy(ub, rx, u_ss, u_rs, 1, 0, d).start()
        else:
            rx[1, h] = ub[1, h]
    for c in range(1, PARTS):
        for d in (2, 1, 3):
            x_copy(ub, rx, u_ss, u_rs, 1, c, d).start()

    def local_back(h, carry):
        for i in range(NCH):
            rows = slice(i * CH, (i + 1) * CH)
            wide = (i + 1) * CH
            attn_s[rows, cols(h)] = (o_s[rows, cols(h)] * invb[rows, :]).astype(BF16)
            inner = mm(gs[rows, cols(h)], v[0:wide, cols(h)], NT)
            dpp[rows, 0:wide] = (inner * wt[h, rows, 0:wide]).astype(BF16)
            grad = mm(dpp[rows, 0:wide], k[0:wide, cols(h)])
            grad = grad + eb[h, rows, :] * mm(gs[rows, cols(h)], str_[0, h], NT)
            gq_s[rows, cols(h)] = grad.astype(BF16)
        for j in range(NCH):
            part = slice(j * CH, (j + 1) * CH)
            gkp[part, cols(h)] = mm(dpp[j * CH :, part], q[j * CH :, cols(h)], TN)
            gvp[part, cols(h)] = mm(pp[h, j * CH :, part], gs[j * CH :, cols(h)], TN)
        return carry

    lax.fori_loop(0, 2, local_back, 0)
    for c in range(PARTS):
        scan_start(1, c)
    lax.fori_loop(2, HEADS, local_back, 0)
    for c in range(PARTS):
        scan_middle(1, c)
    for c in range(PARTS):
        scan_end(1, c)
    for d in (0, 1, 3, 2):
        state_arrive(1, d)
        h = lax.rem(x + XN - d, XN)
        for j in range(NCH):
            part = slice(j * CH, (j + 1) * CH)
            gk_s[part, cols(h)] = (
                gkp[part, cols(h)] + leb[h, part, :] * mm(v[part, cols(h)], str_[1, h], NT)
            ).astype(BF16)
            gv_s[part, cols(h)] = (
                gvp[part, cols(h)] + leb[h, part, :] * mm(k[part, cols(h)], str_[1, h])
            ).astype(BF16)

    for d in range(1, XN):
        c_copy(d).wait_send()
        for n in range(2):
            for c in range(PARTS):
                x_copy(ub, rx, u_ss, u_rs, n, c, d).wait_send()
                x_copy(sts, str_, x_ss, x_rs, n, c, d).wait_send()
    for d in range(1, zn):
        a_copy(d).wait_send()
    for d in range(1, hn):
        h_copy(d).wait_send()
    for n in range(2):
        for copy, steps in ((z1_copy, near), (z2_copy, far)):
            for d in steps:
                @to_later(n, d)
                def _():
                    for c in range(PARTS):
                        copy(n, c, d).wait_send()


def store_kernel(*refs):
    sem = refs[-1]
    copies = [pltpu.make_async_copy(refs[n], refs[4 + n], sem.at[n]) for n in range(4)]
    for copy in copies:
        copy.start()
    for copy in copies:
        copy.wait()


def solution(mesh):
    zn = mesh.shape["seq"] // XN
    hn = mesh.shape["head"]
    near = max(min(3, zn - 1), 1)
    far = max(len(range(4, zn, 4)), 1)
    dma = pltpu.SemaphoreType.DMA

    def per_device(queries, keys, values, cotangent, log_decay, starts):
        big = pltpu.VMEM((TOK, HEADS * DIM), BF16)
        bigf = pltpu.VMEM((TOK, HEADS * DIM), F32)
        col = pltpu.VMEM((HEADS, TOK, DIM), F32)
        row = pltpu.VMEM((HEADS, 1, TOK), F32)
        mat = (DIM, DIM)
        scratch = [
            big, big, big, big, pltpu.VMEM((HEADS, TOK), F32), pltpu.VMEM((1, TOK), jnp.int32),
            pltpu.VMEM((16, TOK), F32), row, row, row, col, col, col,
            pltpu.VMEM((TOK, TOK), F32),
            pltpu.VMEM((HEADS, TOK, TOK), F32),
            pltpu.VMEM((HEADS, TOK, TOK), BF16),
            pltpu.VMEM((TOK, TOK), BF16),
            bigf, big, pltpu.VMEM((HEADS, DIM, TOK), BF16), bigf, bigf,
            pltpu.VMEM((TOK, DIM), F32), pltpu.VMEM((TOK, DIM), F32),
            pltpu.VMEM((TOK, DIM), F32), pltpu.VMEM((TOK, DIM), F32),
            pltpu.VMEM((HEADS, 1, DIM), F32), pltpu.VMEM((XN, 1, DIM), F32),
            pltpu.VMEM((1, 1, DIM), F32), pltpu.VMEM((max(zn - 1, 1), 1, DIM), F32),
            pltpu.VMEM((2, zn, 1, DIM), F32),
            pltpu.VMEM((2, HEADS) + mat, BF16), pltpu.VMEM((2, XN) + mat, BF16),
            pltpu.VMEM(mat, F32),
            pltpu.VMEM((2,) + mat, BF16), pltpu.VMEM((2, near) + mat, BF16),
            pltpu.VMEM((2,) + mat, BF16), pltpu.VMEM((2, far) + mat, BF16),
            pltpu.VMEM(mat, F32),
            pltpu.VMEM((2, XN) + mat, BF16), pltpu.VMEM((2, HEADS) + mat, BF16),
            pltpu.VMEM((8, DIM), F32), pltpu.VMEM((max(hn - 1, 1), 8, DIM), F32),
            dma((6,)),
            dma((3,)), dma((3,)),
            dma((max(zn - 1, 1),)), dma((max(zn - 1, 1),)),
            dma((2, PARTS, 3)), dma((2, PARTS, 3)),
            dma((2, PARTS, near)), dma((2, PARTS, near)),
            dma((2, PARTS, far)), dma((2, PARTS, far)),
            dma((2, PARTS, 3)), dma((2, PARTS, 3)),
            dma((max(hn - 1, 1),)), dma((max(hn - 1, 1),)),
        ]
        out = jax.ShapeDtypeStruct(queries.shape, BF16)
        kept = pltpu.VMEM(queries.shape, BF16)
        hbm = pl.BlockSpec(memory_space=pl.ANY)
        vmem = pl.BlockSpec(memory_space=pltpu.VMEM)
        results = pl.pallas_call(
            functools.partial(kernel, zn, hn),
            out_shape=(kept,) * 4,
            in_specs=[hbm] * 6,
            out_specs=(vmem,) * 4,
            scratch_shapes=scratch,
            compiler_params=pltpu.CompilerParams(
                collective_id=0, has_side_effects=True, vmem_limit_bytes=60 * 1024 * 1024
            ),
        )(queries, keys, values, cotangent, log_decay, starts.reshape(1, TOK))
        return pl.pallas_call(
            store_kernel,
            out_shape=(out,) * 4,
            in_specs=[vmem] * 4,
            out_specs=(hbm,) * 4,
            scratch_shapes=[dma((4,))],
        )(*[pltpu.with_memory_space_constraint(r, pltpu.VMEM) for r in results])

    in_specs = (
        P("seq", "head"),
        P("seq", "head"),
        P("seq", "head"),
        P("seq", "head"),
        P("head", "seq"),
        P("seq"),
    )
    out_specs = (P("seq", "head"), P("seq", "head"), P("seq", "head"), P("seq", "head"))
    return jax.shard_map(
        per_device, mesh=mesh, in_specs=in_specs, out_specs=out_specs, check_vma=False
    )
```

```python
import functools

import jax
import jax.numpy as jnp
from jax import lax
from jax.experimental import pallas as pl
from jax.experimental.pallas import tpu as pltpu
from jax.sharding import PartitionSpec as P

HEADS = 4
DIM = 128
TOK = 512
CH = 128
NCH = TOK // CH
XN = 4
PARTS = 2
PR = DIM // PARTS
EPS = 1e-05
MESH = pl.DeviceIdType.MESH
F32 = jnp.float32
BF16 = jnp.bfloat16
NT = (((1,), (1,)), ((), ()))
TN = (((0,), (0,)), ((), ()))


def mm(a, b, dims=None):
    if dims is None:
        return jnp.dot(a, b, preferred_element_type=F32)
    return lax.dot_general(a, b, dims, preferred_element_type=F32)


def kernel(
    zn, hn,
    q_hbm, k_hbm, v_hbm, c_hbm, ld_hbm, st_hbm,
    attn_s, gq_s, gk_s, gv_s,
    q, k, v, cot, ld_ref, st_ref,
    s16, lrow, enr, ler, lb, eb, leb, bias, wt, pp, dpp, o_s, gs, qd, gkp, gvp,
    acc_s, acc_g, invb, cfb,
    cb, crx, arow, a1r, aw, a2r, cf, coef,
    ub, rx, tf, z1s, z1r, z2s, z2r, w3, sts, str_,
    hs_s, hs_r,
    in_sem, c_ss, c_rs, a1_ss, a1_rs, a2_ss, a2_rs, u_ss, u_rs, z1_ss, z1_rs, z2_ss, z2_rs, x_ss, x_rs, h_ss, h_rs,
):
    full_width = hn * HEADS * DIM
    me = lax.axis_index("seq")
    hd = lax.axis_index("head")
    z = lax.div(me, XN)
    x = lax.rem(me, XN)
    near = [d for d in (1, 2, 3) if d < zn]
    far = [d for d in range(4, zn, 4)]

    def xdev(d):
        return {"seq": z * XN + lax.rem(x + d, XN)}

    def zdev(d):
        return {"seq": lax.rem(z + d, zn) * XN + x}

    def hdev(d):
        return {"head": lax.rem(hd + d, hn)}

    def send(src, dst, ss, rs, dev):
        return pltpu.make_async_remote_copy(
            src_ref=src, dst_ref=dst, send_sem=ss, recv_sem=rs, device_id=dev, device_id_type=MESH
        )

    barrier = pltpu.get_barrier_semaphore()

    def greet(dev):
        pl.semaphore_signal(barrier, inc=1, device_id=dev, device_id_type=MESH)

    def to_later(n, d):
        return pl.when(z + d < zn) if n == 0 else pl.when(z >= d)

    def from_earlier(n, d):
        return pl.when(z >= d) if n == 0 else pl.when(z + d < zn)

    def z_target(n, d):
        return zdev(d) if n == 0 else zdev(zn - d)

    for n in (1, 0):
        for d in (far + near[::-1]):
            @to_later(n, d)
            def _():
                greet(z_target(n, d))
    loads = [
        pltpu.make_async_copy(s, d, in_sem.at[n])
        for n, (s, d) in enumerate(
            ((ld_hbm, ld_ref), (st_hbm, st_ref), (k_hbm, k), (v_hbm, v), (q_hbm, q), (c_hbm, cot))
        )
    ]
    for copy in loads:
        copy.start()
    for d in range(1, XN):
        greet(xdev(d))
    for d in range(1, hn):
        greet(hdev(d))

    loads[0].wait()
    loads[1].wait()
    s16[0:HEADS, :] = ld_ref[...]
    s16[4:5, :] = st_ref[...].astype(F32)
    s16[5:8, :] = jnp.zeros((3, TOK), F32)
    sums = s16[0:8, :]
    lane = lax.broadcasted_iota(jnp.int32, (8, TOK), 1)
    shift = 1
    while shift < TOK:
        sums = sums + jnp.where(lane >= shift, pltpu.roll(sums, shift, 1), 0.0)
        shift *= 2
    lsum = sums[0:HEADS, :]
    count = sums[4:5, :]
    last = sums[:, TOK - 1 : TOK]
    enter = jnp.where(count == 0.0, jnp.exp(lsum), 0.0)
    leave = jnp.where(count == last[4:5], jnp.exp(last[0:HEADS] - lsum), 0.0)
    s16[0:8, :] = sums
    s16[8:12, :] = enter
    s16[12:16, :] = leave
    for h in range(HEADS):
        lrow[h] = lsum[h : h + 1, :]
        enr[h] = enter[h : h + 1, :]
        ler[h] = leave[h : h + 1, :]
        cb[h] = jnp.broadcast_to(enter[h : h + 1, TOK - 1 : TOK], (1, DIM))

    def c_copy(d):
        return send(cb.at[lax.rem(x + d, XN)], crx.at[x], c_ss.at[d - 1], c_rs.at[d - 1], xdev(d))


    def chunk(c):
        return slice(c * PR, (c + 1) * PR)

    def x_copy(src, dst, ss, rs, n, c, d):
        return send(
            src.at[n, lax.rem(x + d, XN), chunk(c)], dst.at[n, x, chunk(c)],
            ss.at[n, c, d - 1], rs.at[n, c, d - 1], xdev(d),
        )

    def x_arrive(src, dst, ss, rs, n, c, d):
        come = lax.rem(x + XN - d, XN)
        send(
            src.at[n, come, chunk(c)], dst.at[n, come, chunk(c)],
            ss.at[n, c, d - 1], rs.at[n, c, d - 1], xdev(d),
        ).wait_recv()

    def cols(h):
        return pl.ds(pl.multiple_of(h * DIM, DIM), DIM)

    loads[2].wait()
    loads[3].wait()
    for d in (2, 1, 3, 0):
        h = lax.rem(x + d, XN)
        kt = k[:, cols(h)].astype(F32).T
        kdec = (kt * ler[h]).astype(BF16)
        ub[0, h] = mm(kdec, v[:, cols(h)]).astype(BF16)
    peers = (XN - 1) + (hn - 1)
    for d in near + far:
        peers = peers + lax.div(z + zn - d, zn) + lax.div(2 * zn - 1 - z - d, zn)
    pl.semaphore_wait(barrier, peers)
    for d in (2, 1, 3):
        c_copy(d).start()
    for c in range(PARTS):
        for d in (2, 1, 3):
            x_copy(ub, rx, u_ss, u_rs, 0, c, d).start()
    crx[x] = cb[x]
    rx[0, x] = ub[0, x]
    columns = s16[...].T
    for h in range(HEADS):
        lb[h] = jnp.broadcast_to(columns[:, h : h + 1], (TOK, DIM))
        eb[h] = jnp.broadcast_to(columns[:, 8 + h : 9 + h], (TOK, DIM))
        leb[h] = jnp.broadcast_to(columns[:, 12 + h : 13 + h], (TOK, DIM))
    row_pos = lax.broadcasted_iota(jnp.int32, (TOK, TOK), 0)
    col_pos = lax.broadcasted_iota(jnp.int32, (TOK, TOK), 1)
    inside = (row_pos >= col_pos) & (columns[:, 4:5] == s16[4:5, :])
    bias[...] = jnp.where(inside, 0.0, -1e30)
    loads[4].wait()

    def intra(h, carry):
        qt = q[:, cols(h)].astype(F32).T
        qd[h] = (qt * enr[h]).astype(BF16)
        for i in range(NCH):
            rows = slice(i * CH, (i + 1) * CH)
            wide = (i + 1) * CH
            scores = mm(q[rows, cols(h)], k[0:wide, cols(h)], NT)
            for j in range(i + 1):
                part = slice(j * CH, (j + 1) * CH)
                gap = jnp.minimum(lb[h, rows, :] - lrow[h, :, part], 0.0)
                weight = jnp.exp(gap + bias[rows, part])
                wt[h, rows, part] = weight
                pp[h, rows, part] = (scores[:, part] * weight).astype(BF16)
            o_s[rows, cols(h)] = mm(pp[h, rows, 0:wide], v[0:wide, cols(h)])
        return carry

    def row_total(n, c):
        rs = chunk(c)
        order = range(XN) if n == 0 else range(XN - 1, -1, -1)
        total = None
        for i in order:
            term = rx[n, i, rs].astype(F32)
            total = term if total is None else total * crx[i] + term
        return total

    def a1_copy(n, d):
        i = near.index(d)
        return send(arow.at[0], a1r.at[n, i], a1_ss.at[n, i], a1_rs.at[n, i], z_target(n, d))

    def a2_copy(n, d):
        i = far.index(d)
        return send(aw.at[n], a2r.at[n, i], a2_ss.at[n, i], a2_rs.at[n, i], z_target(n, d))

    def z1_copy(n, c, d):
        i = near.index(d)
        return send(
            z1s.at[n, chunk(c)], z1r.at[n, i, chunk(c)], z1_ss.at[n, c, i], z1_rs.at[n, c, i], z_target(n, d)
        )

    def z2_copy(n, c, d):
        i = far.index(d)
        return send(
            z2s.at[n, chunk(c)], z2r.at[n, i, chunk(c)], z2_ss.at[n, c, i], z2_rs.at[n, c, i], z_target(n, d)
        )

    def scan_start(n, c):
        for d in (1, 3, 2):
            x_arrive(ub, rx, u_ss, u_rs, n, c, d)
        total = row_total(n, c)
        tf[chunk(c)] = total
        z1s[n, chunk(c)] = total.astype(BF16)
        for d in near[::-1]:
            @to_later(n, d)
            def _():
                z1_copy(n, c, d).start()

    def scan_middle(n, c):
        w3[chunk(c)] = jnp.zeros((PR, DIM), F32)
        if c == 0:
            cf[n] = jnp.ones((1, DIM), F32)
        for d in near:
            @from_earlier(n, d)
            def _():
                if c == 0:
                    a1_copy(n, d).wait_recv()
                    coef[n, d] = cf[n]
                    cf[n] = cf[n] * a1r[n, near.index(d)]
                z1_copy(n, c, d).wait_recv()
                w3[chunk(c)] += coef[n, d] * z1r[n, near.index(d), chunk(c)].astype(F32)
        if far:
            if c == 0:
                aw[n] = arow[0] * cf[n]
            z2s[n, chunk(c)] = (tf[chunk(c)] + arow[0] * w3[chunk(c)]).astype(BF16)
        for d in far:
            @to_later(n, d)
            def _():
                if c == 0:
                    a2_copy(n, d).start()
                z2_copy(n, c, d).start()

    def scan_end(n, c):
        for d in far:
            @from_earlier(n, d)
            def _():
                if c == 0:
                    a2_copy(n, d).wait_recv()
                    coef[n, d] = cf[n]
                    cf[n] = cf[n] * a2r[n, far.index(d)]
                z2_copy(n, c, d).wait_recv()
                w3[chunk(c)] += coef[n, d] * z2r[n, far.index(d), chunk(c)].astype(F32)
        state = w3[chunk(c)]
        order = range(XN) if n == 0 else range(XN - 1, -1, -1)
        for i in order:
            sts[n, i, chunk(c)] = state.astype(BF16)
            state = state * crx[i] + rx[n, i, chunk(c)].astype(F32)
        for d in (2, 1, 3):
            x_copy(sts, str_, x_ss, x_rs, n, c, d).start()
        str_[n, x, chunk(c)] = sts[n, x, chunk(c)]

    def state_arrive(n, d):
        if d:
            for c in range(PARTS):
                x_arrive(sts, str_, x_ss, x_rs, n, c, d)

    lax.fori_loop(0, 1, intra, 0)
    for d in range(1, XN):
        come = lax.rem(x + XN - d, XN)
        send(cb.at[come], crx.at[come], c_ss.at[d - 1], c_rs.at[d - 1], xdev(d)).wait_recv()
    arow[0] = (crx[0] * crx[1]) * (crx[2] * crx[3])

    for n in range(2):
        for d in near:
            @to_later(n, d)
            def _():
                a1_copy(n, d).start()
    for c in range(PARTS):
        scan_start(0, c)
    lax.fori_loop(1, HEADS, intra, 0)
    for c in range(PARTS):
        scan_middle(0, c)
    loads[5].wait()
    for c in range(PARTS):
        scan_end(0, c)
    for d in (0, 1, 3, 2):
        state_arrive(0, d)
        h = lax.rem(x + XN - d, XN)
        for i in range(NCH):
            rows = slice(i * CH, (i + 1) * CH)
            out = o_s[rows, cols(h)] + eb[h, rows, :] * mm(q[rows, cols(h)], str_[0, h])
            o_s[rows, cols(h)] = out
            square = out * out
            along = out * cot[rows, cols(h)].astype(F32)
            if d == 0:
                acc_s[rows, :] = square
                acc_g[rows, :] = along
            else:
                acc_s[rows, :] += square
                acc_g[rows, :] += along
    square_row = jnp.sum(acc_s[...].T, axis=0, keepdims=True)
    along_row = jnp.sum(acc_g[...].T, axis=0, keepdims=True)
    for i in range(NCH):
        hs_s[i : i + 1, :] = square_row[:, i * CH : (i + 1) * CH]
        hs_s[4 + i : 5 + i, :] = along_row[:, i * CH : (i + 1) * CH]

    def h_copy(d):
        return send(hs_s, hs_r.at[d - 1], h_ss.at[d - 1], h_rs.at[d - 1], hdev(d))

    for d in sorted(range(1, hn), key=lambda d: min(d, hn - d), reverse=True):
        h_copy(d).start()
    both = hs_s[...]
    for d in range(1, hn):
        h_copy(d).wait_recv()
        both = both + hs_r[d - 1]
    inverse = lax.rsqrt(both[0:4] / full_width + EPS)
    cubed = inverse * inverse * inverse
    second = cubed * both[4:8] / full_width
    flat = jnp.concatenate([inverse, second], axis=0).T
    for i in range(NCH):
        rows = slice(i * CH, (i + 1) * CH)
        invb[rows, :] = jnp.broadcast_to(flat[:, i : i + 1], (CH, DIM))
        cfb[rows, :] = jnp.broadcast_to(flat[:, 4 + i : 5 + i], (CH, DIM))

    for d in (2, 1, 3, 0):
        h = lax.rem(x + d, XN)
        for i in range(NCH):
            rows = slice(i * CH, (i + 1) * CH)
            gs[rows, cols(h)] = (
                invb[rows, :] * cot[rows, cols(h)].astype(F32) - cfb[rows, :] * o_s[rows, cols(h)]
            ).astype(BF16)
        ub[1, h] = mm(qd[h], gs[:, cols(h)]).astype(BF16)
        if d:
            x_copy(ub, rx, u_ss, u_rs, 1, 0, d).start()
        else:
            rx[1, h] = ub[1, h]
    for c in range(1, PARTS):
        for d in (2, 1, 3):
            x_copy(ub, rx, u_ss, u_rs, 1, c, d).start()

    def local_back(h, carry):
        for i in range(NCH):
            rows = slice(i * CH, (i + 1) * CH)
            wide = (i + 1) * CH
            attn_s[rows, cols(h)] = (o_s[rows, cols(h)] * invb[rows, :]).astype(BF16)
            inner = mm(gs[rows, cols(h)], v[0:wide, cols(h)], NT)
            dpp[rows, 0:wide] = (inner * wt[h, rows, 0:wide]).astype(BF16)
            grad = mm(dpp[rows, 0:wide], k[0:wide, cols(h)])
            grad = grad + eb[h, rows, :] * mm(gs[rows, cols(h)], str_[0, h], NT)
            gq_s[rows, cols(h)] = grad.astype(BF16)
        for j in range(NCH):
            part = slice(j * CH, (j + 1) * CH)
            gkp[part, cols(h)] = mm(dpp[j * CH :, part], q[j * CH :, cols(h)], TN)
            gvp[part, cols(h)] = mm(pp[h, j * CH :, part], gs[j * CH :, cols(h)], TN)
        return carry

    lax.fori_loop(0, 2, local_back, 0)
    for c in range(PARTS):
        scan_start(1, c)
    lax.fori_loop(2, HEADS, local_back, 0)
    for c in range(PARTS):
        scan_middle(1, c)
    for c in range(PARTS):
        scan_end(1, c)
    for d in (0, 1, 3, 2):
        state_arrive(1, d)
        h = lax.rem(x + XN - d, XN)
        for j in range(NCH):
            part = slice(j * CH, (j + 1) * CH)
            gk_s[part, cols(h)] = (
                gkp[part, cols(h)] + leb[h, part, :] * mm(v[part, cols(h)], str_[1, h], NT)
            ).astype(BF16)
            gv_s[part, cols(h)] = (
                gvp[part, cols(h)] + leb[h, part, :] * mm(k[part, cols(h)], str_[1, h])
            ).astype(BF16)

    for d in range(1, XN):
        c_copy(d).wait_send()
        for n in range(2):
            for c in range(PARTS):
                x_copy(ub, rx, u_ss, u_rs, n, c, d).wait_send()
                x_copy(sts, str_, x_ss, x_rs, n, c, d).wait_send()
    for d in range(1, hn):
        h_copy(d).wait_send()
    for n in range(2):
        for copy, small, steps in ((z1_copy, a1_copy, near), (z2_copy, a2_copy, far)):
            for d in steps:
                @to_later(n, d)
                def _():
                    small(n, d).wait_send()
                    for c in range(PARTS):
                        copy(n, c, d).wait_send()


def store_kernel(*refs):
    sem = refs[-1]
    copies = [
        pltpu.make_async_copy(refs[n].at[pl.ds(i * CH, CH)], refs[4 + n].at[pl.ds(i * CH, CH)], sem.at[n, i])
        for n in range(4)
        for i in range(NCH)
    ]
    for copy in copies:
        copy.start()
    for copy in copies:
        copy.wait()


def solution(mesh):
    zn = mesh.shape["seq"] // XN
    hn = mesh.shape["head"]
    near = max(min(3, zn - 1), 1)
    far = max(len(range(4, zn, 4)), 1)
    dma = pltpu.SemaphoreType.DMA

    def per_device(queries, keys, values, cotangent, log_decay, starts):
        big = pltpu.VMEM((TOK, HEADS * DIM), BF16)
        bigf = pltpu.VMEM((TOK, HEADS * DIM), F32)
        col = pltpu.VMEM((HEADS, TOK, DIM), F32)
        row = pltpu.VMEM((HEADS, 1, TOK), F32)
        mat = (DIM, DIM)
        scratch = [
            big, big, big, big, pltpu.VMEM((HEADS, TOK), F32), pltpu.VMEM((1, TOK), jnp.int32),
            pltpu.VMEM((16, TOK), F32), row, row, row, col, col, col,
            pltpu.VMEM((TOK, TOK), F32),
            pltpu.VMEM((HEADS, TOK, TOK), F32),
            pltpu.VMEM((HEADS, TOK, TOK), BF16),
            pltpu.VMEM((TOK, TOK), BF16),
            bigf, big, pltpu.VMEM((HEADS, DIM, TOK), BF16), bigf, bigf,
            pltpu.VMEM((TOK, DIM), F32), pltpu.VMEM((TOK, DIM), F32),
            pltpu.VMEM((TOK, DIM), F32), pltpu.VMEM((TOK, DIM), F32),
            pltpu.VMEM((HEADS, 1, DIM), F32), pltpu.VMEM((XN, 1, DIM), F32),
            pltpu.VMEM((1, 1, DIM), F32), pltpu.VMEM((2, near, 1, DIM), F32),
            pltpu.VMEM((2, 1, DIM), F32), pltpu.VMEM((2, far, 1, DIM), F32),
            pltpu.VMEM((2, 1, DIM), F32),
            pltpu.VMEM((2, zn, 1, DIM), F32),
            pltpu.VMEM((2, HEADS) + mat, BF16), pltpu.VMEM((2, XN) + mat, BF16),
            pltpu.VMEM(mat, F32),
            pltpu.VMEM((2,) + mat, BF16), pltpu.VMEM((2, near) + mat, BF16),
            pltpu.VMEM((2,) + mat, BF16), pltpu.VMEM((2, far) + mat, BF16),
            pltpu.VMEM(mat, F32),
            pltpu.VMEM((2, XN) + mat, BF16), pltpu.VMEM((2, HEADS) + mat, BF16),
            pltpu.VMEM((8, DIM), F32), pltpu.VMEM((max(hn - 1, 1), 8, DIM), F32),
            dma((6,)),
            dma((3,)), dma((3,)),
            dma((2, near)), dma((2, near)),
            dma((2, far)), dma((2, far)),
            dma((2, PARTS, 3)), dma((2, PARTS, 3)),
            dma((2, PARTS, near)), dma((2, PARTS, near)),
            dma((2, PARTS, far)), dma((2, PARTS, far)),
            dma((2, PARTS, 3)), dma((2, PARTS, 3)),
            dma((max(hn - 1, 1),)), dma((max(hn - 1, 1),)),
        ]
        out = jax.ShapeDtypeStruct(queries.shape, BF16)
        kept = pltpu.VMEM(queries.shape, BF16)
        hbm = pl.BlockSpec(memory_space=pl.ANY)
        vmem = pl.BlockSpec(memory_space=pltpu.VMEM)
        results = pl.pallas_call(
            functools.partial(kernel, zn, hn),
            out_shape=(kept,) * 4,
            in_specs=[hbm] * 6,
            out_specs=(vmem,) * 4,
            scratch_shapes=scratch,
            compiler_params=pltpu.CompilerParams(
                collective_id=0, has_side_effects=True, vmem_limit_bytes=60 * 1024 * 1024
            ),
        )(queries, keys, values, cotangent, log_decay, starts.reshape(1, TOK))
        return pl.pallas_call(
            store_kernel,
            out_shape=(out,) * 4,
            in_specs=[vmem] * 4,
            out_specs=(hbm,) * 4,
            scratch_shapes=[dma((4, NCH))],
        )(*[pltpu.with_memory_space_constraint(r, pltpu.VMEM) for r in results])

    in_specs = (
        P("seq", "head"),
        P("seq", "head"),
        P("seq", "head"),
        P("seq", "head"),
        P("head", "seq"),
        P("seq"),
    )
    out_specs = (P("seq", "head"), P("seq", "head"), P("seq", "head"), P("seq", "head"))
    return jax.shard_map(
        per_device, mesh=mesh, in_specs=in_specs, out_specs=out_specs, check_vma=False
    )
```
